32 devices in a mesh: dp: 8 (over y, x, core), mp: 4 (over z).
Axes of the slice: x: 2, y: 2, z: 4, core: 2. Of those that a mesh axis runs over, the one named last changes fastest.
Arguments:
- target_states: bfloat16 [1024, 4096], P('dp', 'mp')
- target_gain: float32 [4096], replicated, may hold values from 0.1 to 1.9
- target_head: bfloat16 [4096, 128256], P(None, ('dp', 'mp'))
- reference_states: bfloat16 [1024, 2048], P(('dp', 'mp'))
- reference_gain: float32 [2048], replicated, may hold values from 0.1 to 1.9
- reference_head: bfloat16 [2048, 128256], P(None, ('dp', 'mp'))
- token_ids: int32 [1024], P('dp'), may hold values from 0 to 128255
- reference_order: int32 [8], replicated, may hold values from 0 to 7, each once
Outputs:
- target_loss: float32 [1024], P('dp')
- reference_loss: float32 [1024], P('dp')
- reducible: float32 [8], P('dp')
The draws below stay inside these ranges and needn't reach their ends.
Inputs may be any that keep to these rules, and one draw needn't show every extreme that they name: reference_states rows s * 128 to s * 128 + 127 belong to candidate sequence reference_order[s].
All inputs are finite; a program needn't handle non-finite values.
Results may differ from the reference program's by a relative error of at most 0.0041.
Values may be sent and summed in bfloat16 or wider, within the bound.
A program may use at most 128 MiB of HBM per device.

```python
import math
import jax
import jax.numpy as jnp
import numpy as np
from jax import lax

D = 4096
DR = 2048
VOCAB = 128256
LENGTH = 128
SEQS = 8
TOKENS = 1024


def drawn_head(key, offset, breadth):
    raw_draw = jnp.clip(jax.random.normal(jax.random.fold_in(key, offset), (breadth, VOCAB), jnp.float32), -6.0, 6.0)
    column_ramp = 0.75 + 0.5 * jnp.arange(VOCAB, dtype=jnp.float32) / VOCAB
    return (raw_draw, column_ramp)


def entries_head(key, offset, breadth):
    raw_draw, column_ramp = drawn_head(key, offset, breadth)
    return raw_draw * (3.0 * column_ramp / math.sqrt(breadth))[None, :]


def drawn_states(key, offset, breadth):
    base_key = jax.random.fold_in(key, offset + 5)
    return jnp.clip(jax.random.normal(jax.random.fold_in(base_key, 1), (TOKENS, breadth), jnp.float32), -6.0, 6.0)


def draw_target_head(key, part):
    return entries_head(key, 10, D).astype(jnp.bfloat16)


def draw_reference_head(key, part):
    return entries_head(key, 20, DR).astype(jnp.bfloat16)


def draw_target_states(key, part):
    return drawn_states(key, 10, D).astype(jnp.bfloat16)


def draw_reference_states(key, part):
    return drawn_states(key, 20, DR).astype(jnp.bfloat16)


def with_ends(values, key, least, high):
    place = [jax.random.randint(jax.random.fold_in(key, axis), (), 0, length) for axis, length in enumerate(values.shape)]
    main_axis = values.shape.index(max(values.shape))
    next_to = place[:main_axis] + [(place[main_axis] + 1) % values.shape[main_axis]] + place[main_axis + 1:]
    return values.at[tuple(place)].set(least).at[tuple(next_to)].set(high)


def wide_ids(stream_key, shape, amount, lean):
    loads = [min(1 << octave, amount + 1 - (1 << octave)) * (1 << 20) // math.isqrt((1 << octave) ** lean) + 1 for octave in range((amount + 1).bit_length()) if 1 << octave <= amount]
    deviation = 1 + sum(loads) // (1 << 30)
    table = np.cumsum(np.array([max(1, weight // deviation) for weight in loads]))
    pick = jax.random.randint(jax.random.fold_in(stream_key, 1), shape, 0, int(table[len(loads) - 1]))
    start = jnp.left_shift(1, jnp.searchsorted(jnp.asarray(table, jnp.int32), pick, side="right").astype(jnp.int32))
    grade = start - 1 + jax.random.randint(jax.random.fold_in(stream_key, 4), shape, 0, 1 << 30) % jnp.minimum(start, amount + 1 - start)
    return jax.random.permutation(jax.random.fold_in(stream_key, 2), amount)[grade].astype(jnp.int32)


def setup_inputs(seed: int = 0) -> dict:
    seeds = jax.random.split(jax.random.key(seed), 9)
    return {
        "target_states": draw_target_states(jax.random.fold_in(seeds[8], 71), 0),
        "target_gain": jnp.clip(1.0 + 0.18 * jax.random.normal(seeds[1], (D,), jnp.float32), 0.1, 1.9),
        "target_head": draw_target_head(jax.random.fold_in(seeds[8], 71), 0),
        "reference_states": draw_reference_states(jax.random.fold_in(seeds[8], 71), 0),
        "reference_gain": jnp.clip(1.0 + 0.18 * jax.random.normal(seeds[4], (DR,), jnp.float32), 0.1, 1.9),
        "reference_head": draw_reference_head(jax.random.fold_in(seeds[8], 71), 0),
        "token_ids": with_ends(wide_ids(seeds[6], (TOKENS,), VOCAB, 2), jax.random.fold_in(seeds[6], 3), 0, VOCAB - 1).astype(jnp.int32),
        "reference_order": jax.random.permutation(seeds[7], SEQS).astype(jnp.int32),
    }


EPSILON = 1e-05

def normalize(states, gain):
    values = states.astype(jnp.float32)
    factor = lax.rsqrt(lax.optimization_barrier(jnp.mean(values * values, axis=1, keepdims=True)) + EPSILON)
    return (values * factor * gain.astype(jnp.float32)[None, :]).astype(jnp.bfloat16)

def losses(normed, head, ids):
    count = normed.shape[0]
    blocking = math.gcd(count, 256)

    def one_block(packed):
        rows_x, rows_id = packed
        logits = jnp.dot(rows_x, head, preferred_element_type=jnp.float32)
        peak_val = lax.optimization_barrier(jnp.max(logits, axis=1))
        log_total = peak_val + jnp.log(lax.optimization_barrier(jnp.sum(jnp.exp(logits - peak_val[:, None]), axis=1)))
        chosen = jnp.take_along_axis(logits, rows_id[:, None], axis=1)[:, 0]
        return log_total - chosen
    stacked = lax.map(one_block, (normed.reshape(-1, blocking, normed.shape[1]), ids.reshape(-1, blocking)))
    return stacked.reshape(count)

def reference(target_states, target_gain, target_head, reference_states, reference_gain, reference_head, token_ids, reference_order):
    target_loss = losses(normalize(target_states, target_gain), target_head, token_ids)
    seq_ids = token_ids.reshape(SEQS, LENGTH)
    reference_ids = jnp.take(seq_ids, reference_order.astype(jnp.int32), axis=0).reshape(TOKENS)
    rows_loss = losses(normalize(reference_states, reference_gain), reference_head, reference_ids)
    matches = (reference_order[:, None] == jnp.arange(SEQS, dtype=jnp.int32)[None, :]).astype(jnp.float32)
    reference_loss = lax.optimization_barrier(jnp.sum(matches[:, :, None] * rows_loss.reshape(SEQS, LENGTH)[:, None, :], axis=0)).reshape(TOKENS)
    reducible = lax.optimization_barrier(jnp.mean((target_loss - reference_loss).reshape(SEQS, LENGTH), axis=1))
    return (target_loss, reference_loss, reducible)
```

```python
import functools

import jax
import jax.numpy as jnp
from jax import lax
from jax.experimental import pallas as pl
from jax.experimental.pallas import tpu as pltpu
from jax.sharding import PartitionSpec as P

EPSILON = 1e-05
MESH = pl.DeviceIdType.MESH
LANES = 128
FAR = 1 << 29
LEAST = -0.7 * 3.4e38


def flip(p, mask, bits):
    for j in range(bits):
        if (mask >> j) & 1:
            unit = 1 << j
            p = p + unit * (1 - 2 * ((p // unit) % 2))
    return p


def reverse(v, bits):
    return sum(((v >> j) & 1) << (bits - 1 - j) for j in range(bits))


def to_rows(column_block):
    return jnp.transpose(column_block)[0:8, :]


def to_column(row):
    return jnp.transpose(jnp.broadcast_to(row, (LANES, LANES)))


def kernel(
    cfg, order, inverse, ts, tg, rs, rg, ids8, th, rh, out,
    xt, xr, wfull, wlast, l0, l1, mx, sm, ht, idb, idall, ssend, sall, stat, sbuf, rbuf,
    send_sem, plane_sem, part_sem, ids_ssem, ids_rsem, ss_ssem, ss_rsem, fin_ssem, fin_rsem, wsem, lsem,
):
    dp, mp, planes, bits, chunk, tile, full, last = (
        cfg["dp"], cfg["mp"], cfg["planes"], cfg["bits"], cfg["chunk"], cfg["tile"], cfg["full"], cfg["last"]
    )
    half = tile // 2
    n = dp * mp
    d, z = lax.axis_index("dp"), lax.axis_index("mp")
    me = d * mp + z
    p, c = d // 2, d % 2
    other = 1 - c
    partner = (2 * p + other, z)
    rows, feats = ts.shape
    depth_t, depth_r = xt.shape[1], xr.shape[1]
    rrows = rs.shape[0]
    width = th.shape[1]
    base = me * width

    barrier = pltpu.get_barrier_semaphore()

    def greet(j, _):
        t = (me + j) % n
        pl.semaphore_signal(barrier, inc=1, device_id=(t // mp, t % mp), device_id_type=MESH)
        return 0

    lax.fori_loop(1, n, greet, 0)

    def blend(a, b):
        return a * (1 - c) + b * c

    def plane_of(v, core):
        a, b = flip(p, v, bits), flip(p, reverse(v, bits), bits)
        return a * (1 - core) + b * core

    def block(model, plane, core, zz):
        if model == 0:
            start = pl.multiple_of(((plane * 2 + core) * mp + zz) * rrows, rrows)
            return xr.at[pl.ds(start, rrows), :]
        start = pl.multiple_of((plane * 2 + core) * rows, rows)
        lane = pl.multiple_of(zz * feats, LANES)
        return xt.at[pl.ds(start, rows), pl.ds(lane, feats)]

    sent = []

    def push(model, ref, rsem, dev):
        pltpu.make_async_remote_copy(
            src_ref=ref, dst_ref=ref, send_sem=send_sem.at[len(sent)], recv_sem=rsem,
            device_id=dev, device_id_type=MESH,
        ).start()
        sent.append(model)

    def arrived(ref, rsem):
        pltpu.make_async_remote_copy(
            src_ref=ref, dst_ref=ref, send_sem=send_sem.at[0], recv_sem=rsem,
            device_id=partner, device_id_type=MESH,
        ).wait_recv()

    def slot(model, v, i):
        return (model * planes + v) * mp + i

    def event(model, v, i):
        zz = (z + i) % mp
        ref = block(model, plane_of(v, c), c, zz)
        if (v, i) != (0, 0):
            arrived(ref, plane_sem.at[slot(model, v, i)])
        else:
            for k in range(1, mp):
                push(model, ref, plane_sem.at[slot(model, 0, mp - k)], (d, (z + k) % mp))
        high = v.bit_length()
        for k in range(high, bits):
            near = blend(flip(p, 1 << k, bits), flip(p, 1 << (bits - 1 - k), bits))
            push(model, ref, plane_sem.at[slot(model, v | (1 << k), i)], (2 * near + c, z))
        push(model, ref, part_sem.at[slot(model, v, i)], partner)

    def partner_ready(model, r):
        v = r * (1 - other) + reverse(r, bits) * other
        plane = flip(p, r, bits)
        for i in range(mp):
            arrived(block(model, plane, other, (z + i) % mp), part_sem.at[(model * planes + v) * mp + i])

    models = [0] * (planes // 2) + [1] * (planes // 2)

    def full_copy(model, i, s):
        head, depth = (rh, depth_r) if model == 0 else (th, depth_t)
        return pltpu.make_async_copy(
            head.at[:, pl.ds(pl.multiple_of(i * tile, LANES), tile)], wfull.at[s, pl.ds(0, depth), :], wsem.at[s]
        )

    def last_copy(model):
        head, depth = (rh, depth_r) if model == 0 else (th, depth_t)
        return pltpu.make_async_copy(
            head.at[:, pl.ds(full * tile, last)], wlast.at[pl.ds(0, depth), :], lsem.at[0]
        )

    full_copy(0, 0, 0).start()
    last_copy(0).start()

    values = ts[...].astype(jnp.float32)
    mine = jnp.sum(values * values, axis=1, keepdims=True)
    ssend[...] = to_rows(jnp.broadcast_to(mine, (rows, LANES)))
    rvals = rs[...].astype(jnp.float32)
    rfac = lax.rsqrt(jnp.sum(rvals * rvals, axis=1, keepdims=True) / depth_r + EPSILON)
    own_r = pl.multiple_of(me * rrows, rrows)
    xr[pl.ds(own_r, rrows), :] = (rvals * rfac * rg[...]).astype(jnp.bfloat16)
    idall[d] = ids8[...]

    pl.semaphore_wait(barrier, n - 1)

    small = []
    for k in range(1, mp):
        cp = pltpu.make_async_remote_copy(
            src_ref=ssend, dst_ref=sall.at[mp - k], send_sem=ss_ssem.at[k], recv_sem=ss_rsem.at[mp - k],
            device_id=(d, (z + k) % mp), device_id_type=MESH,
        )
        cp.start()
        small.append(cp)
    event(0, 0, 0)
    for k in range(1, dp):
        cp = pltpu.make_async_remote_copy(
            src_ref=ids8, dst_ref=idall.at[d], send_sem=ids_ssem.at[k], recv_sem=ids_rsem.at[dp - k],
            device_id=((d + k) % dp, z), device_id_type=MESH,
        )
        cp.start()
        small.append(cp)

    total = ssend[...]
    for k in range(1, mp):
        pltpu.make_async_remote_copy(
            src_ref=ssend, dst_ref=sall.at[k], send_sem=ss_ssem.at[k], recv_sem=ss_rsem.at[k],
            device_id=partner, device_id_type=MESH,
        ).wait_recv()
        total = total + sall[k]
    factor = to_column(lax.rsqrt(total / depth_t + EPSILON)[0:1, :])
    for g in range(feats // LANES):
        at = pl.multiple_of(z * feats + g * LANES, LANES)
        part = ts[:, g * LANES : (g + 1) * LANES].astype(jnp.float32)
        xt[pl.ds(pl.multiple_of(d * rows, rows), rows), pl.ds(at, LANES)] = (
            part * factor * tg[:, pl.ds(at, LANES)]
        ).astype(jnp.bfloat16)

    for i in range(1, mp):
        event(0, 0, i)
    event(1, 0, 0)

    for k in range(1, dp):
        src = (d + k) % dp
        pltpu.make_async_remote_copy(
            src_ref=ids8, dst_ref=idall.at[src], send_sem=ids_ssem.at[k], recv_sem=ids_rsem.at[k],
            device_id=partner, device_id_type=MESH,
        ).wait_recv()

    vs = sorted(range(planes), key=lambda v: (bin(v).count("1"), v))

    def needed(a):
        want = [2 * a, 2 * a + 1, reverse(2 * a, bits), reverse(2 * a + 1, bits)]
        return max(vs.index(v) for v in want) + 1

    count = planes // 2
    todo = {0: [(0, v, i) for v in vs[1:] for i in range(mp)], 1: [(1, v, i) for v in vs for i in range(mp)][1:]}

    def flush(model, a):
        keep = set(vs[: needed(a)])
        while any(v in keep for _, v, _ in todo[model]):
            event(*todo[model].pop(0))

    lane = lax.broadcasted_iota(jnp.int32, (1, LANES), 1)
    strip = 64

    def stats(buf, offset, wide):
        groups = -(-wide // LANES)
        for r in range(0, chunk, strip):
            at = pl.ds(r, strip)
            m_old = mx[at, :]
            pieces = []
            for g in range(groups):
                piece = buf[at, g * LANES : (g + 1) * LANES]
                if (g + 1) * LANES > wide:
                    piece = jnp.where(lane < wide - g * LANES, piece, LEAST)
                pieces.append(piece)
            m_new = functools.reduce(jnp.maximum, pieces, m_old)
            rel = idb[at, :] - offset
            tot = sm[at, :] * jnp.exp(m_old - m_new)
            hit = ht[at, :]
            for g in range(groups):
                tot = tot + jnp.exp(pieces[g] - m_new)
                match = rel == lane + g * LANES
                if (g + 1) * LANES > wide:
                    match = match & (lane < wide - g * LANES)
                hit = hit + jnp.where(match, pieces[g], 0.0)
            mx[at, :] = m_new
            sm[at, :] = tot
            ht[at, :] = hit

    step = 0
    for index, model in enumerate(models):
        a = index % count
        x, depth = (xr, depth_r) if model == 0 else (xt, depth_t)
        flush(model, a)
        for r in (2 * a, 2 * a + 1):
            partner_ready(model, r)
        plane = flip(p, 2 * a, bits)
        first = (plane // 2) * 2
        start = pl.multiple_of(first * 2 * rows, chunk)
        for s in range(chunk // LANES):
            which = first * 2 + s
            src = order[which] if model == 0 else which
            idb[s * LANES : (s + 1) * LANES, :] = to_column(idall[src][0:1, :]) - base
        mx[...] = jnp.full(mx.shape, LEAST, jnp.float32)
        sm[...] = jnp.zeros(sm.shape, jnp.float32)
        ht[...] = jnp.zeros(ht.shape, jnp.float32)
        l1[...] = jnp.full(l1.shape, LEAST, jnp.float32)

        if model == 0 and a + 1 < count:
            ahead = todo[0] + todo[1][: mp - 1]
            todo[1] = todo[1][mp - 1 :]
            todo[0] = []
        elif model == 0:
            keep = set(vs[: needed(0)])
            ahead = [e for e in todo[1] if e[1] in keep]
            todo[1] = todo[1][len(ahead) :]
        else:
            ahead, todo[1] = todo[1], []
        if index > 0:
            last_copy(model).start()
        upcoming = models[index + 1] if index + 1 < len(models) else None
        at_step = {}
        for e, item in enumerate(ahead):
            at_step.setdefault(e * full // max(len(ahead), 1), []).append(item)

        def body(i, _, model=model, x=x, depth=depth, start=start, step=step, upcoming=upcoming, at_step=at_step):
            s = (step + i) % 2
            full_copy(model, i, s).wait()

            @pl.when(i + 1 < full)
            def _():
                full_copy(model, i + 1, 1 - s).start()

            if upcoming is not None:
                @pl.when(i + 1 == full)
                def _():
                    full_copy(upcoming, 0, 1 - s).start()

            for when, items in at_step.items():
                @pl.when(i == when)
                def _():
                    for item in items:
                        event(*item)

            lhs = x.at[pl.ds(start, chunk), :]
            l0[...] = jnp.dot(lhs[...], wfull[s, 0:depth, 0:half], preferred_element_type=jnp.float32)
            stats(l1, jnp.where(i == 0, FAR, i * tile - half), half)
            l1[...] = jnp.dot(lhs[...], wfull[s, 0:depth, half:tile], preferred_element_type=jnp.float32)
            stats(l0, i * tile, half)
            return 0

        lax.fori_loop(0, full, body, 0)
        step += full
        lhs = x.at[pl.ds(start, chunk), :]
        last_copy(model).wait()
        l0[...] = jnp.dot(lhs[...], wlast[0:depth, 0:half], preferred_element_type=jnp.float32)
        stats(l1, full * tile - half, half)
        l1[:, 0 : last - half] = jnp.dot(lhs[...], wlast[0:depth, half:last], preferred_element_type=jnp.float32)
        stats(l0, full * tile, half)
        stats(l1, full * tile + half, last - half)
        for s in range(chunk // LANES):
            at = pl.ds(s * LANES, LANES)
            top = jnp.max(mx[at, :], axis=1, keepdims=True)
            tot = jnp.sum(sm[at, :] * jnp.exp(mx[at, :] - top), axis=1, keepdims=True)
            hit = jnp.sum(ht[at, :], axis=1, keepdims=True)
            mixed = jnp.where(lane == 0, top, jnp.where(lane == 1, tot, hit))
            stat[model, first * 2 + s] = to_rows(mixed)

    for k in range(dp):
        sbuf[k, 0:8, :] = stat[1, k]
        sbuf[k, 8:16, :] = stat[0, inverse[k]]

    def deliver(k):
        t = (me + k) % n
        return pltpu.make_async_remote_copy(
            src_ref=sbuf.at[t // mp], dst_ref=rbuf.at[n - k], send_sem=fin_ssem.at[k], recv_sem=fin_rsem.at[n - k],
            device_id=(t // mp, t % mp), device_id_type=MESH,
        )

    def start_one(k, _):
        deliver(k).start()
        return 0

    lax.fori_loop(1, n, start_one, 0)
    rbuf[0] = sbuf[d]
    for k, model in enumerate(sent):
        ref = block(model, p, c, z)
        pltpu.make_async_remote_copy(
            src_ref=ref, dst_ref=ref, send_sem=send_sem.at[k], recv_sem=plane_sem.at[0],
            device_id=partner, device_id_type=MESH,
        ).wait_send()
    for copy in small:
        copy.wait_send()

    def wait_one(k, _):
        deliver(k).wait()
        return 0

    lax.fori_loop(1, n, wait_one, 0)

    parts = []
    for off in (0, 8):
        top = rbuf[0, off : off + 1, :]
        for k in range(1, n):
            top = jnp.maximum(top, rbuf[k, off : off + 1, :])
        tot = jnp.zeros_like(top)
        hit = jnp.zeros_like(top)
        for k in range(n):
            tot = tot + rbuf[k, off + 1 : off + 2, :] * jnp.exp(rbuf[k, off : off + 1, :] - top)
            hit = hit + rbuf[k, off + 2 : off + 3, :]
        parts.append(top + jnp.log(tot) - hit)
    loss_t, loss_r = parts
    mean = jnp.sum(loss_t - loss_r, axis=1, keepdims=True) / rows
    out[0:1, :] = loss_t
    out[1:2, :] = loss_r
    out[2:3, :] = jnp.broadcast_to(mean, (1, LANES))
    out[3:8, :] = jnp.zeros((5, LANES), jnp.float32)


def shards(dp, mp, ts, tg, th, rs, rg, rh, ids, order):
    rows, feats = ts.shape
    width = th.shape[1]
    depth_t, depth_r = th.shape[0], rh.shape[0]
    tokens = rows * dp
    planes = dp // 2
    bits = planes.bit_length() - 1
    chunk = 4 * rows
    tile = 512
    full = (width - 1) // tile
    last = width - full * tile
    cfg = dict(dp=dp, mp=mp, planes=planes, bits=bits, chunk=chunk, tile=tile, full=full, last=last)
    n = dp * mp
    seqs = order.shape[0]
    inverse = jnp.sum(
        jnp.where(order[:, None] == jnp.arange(seqs, dtype=jnp.int32)[None, :],
                  jnp.arange(seqs, dtype=jnp.int32)[:, None], 0), axis=0).astype(jnp.int32)
    ids8 = jnp.broadcast_to(ids[None, :], (8, rows))
    hops = sum(bits - v.bit_length() + 1 for v in range(planes)) * mp + mp - 1
    f32 = jnp.float32
    vmem = pl.BlockSpec(memory_space=pltpu.VMEM)
    smem = pl.BlockSpec(memory_space=pltpu.SMEM)
    anyspace = pl.BlockSpec(memory_space=pl.ANY)
    dma = pltpu.SemaphoreType.DMA
    out = pl.pallas_call(
        functools.partial(kernel, cfg),
        out_shape=jax.ShapeDtypeStruct((8, LANES), f32),
        in_specs=[smem, smem, vmem, vmem, vmem, vmem, vmem, anyspace, anyspace],
        out_specs=vmem,
        scratch_shapes=[
            pltpu.VMEM((tokens, depth_t), jnp.bfloat16),
            pltpu.VMEM((tokens, depth_r), jnp.bfloat16),
            pltpu.VMEM((2, depth_t, tile), jnp.bfloat16),
            pltpu.VMEM((depth_t, last), jnp.bfloat16),
            pltpu.VMEM((chunk, tile // 2), f32),
            pltpu.VMEM((chunk, tile // 2), f32),
            pltpu.VMEM((chunk, LANES), f32),
            pltpu.VMEM((chunk, LANES), f32),
            pltpu.VMEM((chunk, LANES), f32),
            pltpu.VMEM((chunk, LANES), jnp.int32),
            pltpu.VMEM((dp, 8, rows), jnp.int32),
            pltpu.VMEM((8, LANES), f32),
            pltpu.VMEM((mp, 8, LANES), f32),
            pltpu.VMEM((2, dp, 8, LANES), f32),
            pltpu.VMEM((dp, 16, LANES), f32),
            pltpu.VMEM((n, 16, LANES), f32),
            dma((2 * hops,)),
            dma((2 * planes * mp,)),
            dma((2 * planes * mp,)),
            dma((dp,)),
            dma((dp,)),
            dma((mp,)),
            dma((mp,)),
            dma((n,)),
            dma((n,)),
            dma((2,)),
            dma((1,)),
        ],
        compiler_params=pltpu.CompilerParams(
            collective_id=0, has_side_effects=True, vmem_limit_bytes=60 * 1024 * 1024
        ),
    )(order, inverse, ts, tg[None, :], rs, rg[None, :], ids8, th, rh)
    return out[0], out[1], out[2, 0 : rows // LANES]


def solution(mesh):
    placed = (
        P("dp", "mp"),
        P(),
        P(None, ("dp", "mp")),
        P(("dp", "mp"), None),
        P(),
        P(None, ("dp", "mp")),
        P("dp"),
        P(),
    )
    return jax.shard_map(
        functools.partial(shards, mesh.shape["dp"], mesh.shape["mp"]),
        mesh=mesh, in_specs=placed, out_specs=(P("dp"), P("dp"), P("dp")), check_vma=False,
    )
```
